1024 devices in a mesh: cuts: 16 (over z_lo), energy: 8 (over z_hi, y), group: 8 (over x, core).
Axes of the slice: x: 4, y: 4, z: 32 (z_hi: 2, z_lo: 16; z = z_hi * 16 + z_lo), core: 2. Of those that a mesh axis runs over, the one named last changes fastest.
Arguments:
- transfer: float32 [8, 48, 512, 512], P('energy', 'cuts'), may hold values from -1.5 to 1.5
- source: float32 [8, 24576, 1024], P('energy', 'cuts', 'group'), may hold values from -4 to 4
- coupling: bfloat16 [512, 512], replicated, may hold values from -0.25 to 0.25
- strength: float32 [8], replicated, may hold values from 0.2 to 1
- mode_shift: int32 [8], replicated, may hold values from 0 to 7, as said below
Outputs:
- green: float32 [8, 24576, 1024], P('energy', 'cuts', 'group')
- scattered: float32 [8, 24576, 1024], P('energy', 'cuts', 'group')
The draws below stay inside these ranges and needn't reach their ends.
Inputs may be any that keep to these rules, and one draw needn't show every extreme that they name: `mode_shift`: every energy offset of 0 to 7 is taken by at least one mode.
All inputs are finite; a program needn't handle non-finite values.
Results may differ from the reference program's by a relative error of at most 0.0035.
Values sent between devices are 32-bit elements; how exact they have to be, the bound alone decides.
A program may use at most 64 MiB of HBM per device.

```python
import math
import jax
import jax.numpy as jnp
from jax import lax

ORB = 512
MODES = 8
ENERGIES = 8
CHAIN_BLOCKS = 48
COLUMNS = 1024


def draw_transfer(key, part):
    random_keys = jax.random.split(key, 7)
    slow_share = 0.5
    slow = jax.random.bernoulli(random_keys[0], slow_share, (ENERGIES, 1, ORB))
    slow_rate = jax.random.uniform(random_keys[1], (ENERGIES, 1, ORB), jnp.float32, 0.2, 0.8) / CHAIN_BLOCKS
    fast_rate = jax.random.uniform(random_keys[2], (ENERGIES, 1, ORB), jnp.float32, 0.5, 1.2)
    rate = jnp.where(slow, slow_rate, fast_rate)
    spread = jnp.exp(jax.random.uniform(random_keys[3], (ENERGIES, CHAIN_BLOCKS, ORB), jnp.float32, -0.35, 0.35))
    spike_location = jax.random.randint(random_keys[4], (2,), 0, CHAIN_BLOCKS)
    spike_event = jnp.any(jnp.arange(CHAIN_BLOCKS)[:, None] == spike_location[None, :], axis=1)
    decay_loss = jax.random.uniform(random_keys[5], (ENERGIES, CHAIN_BLOCKS, ORB), jnp.float32, 0.2, 0.4)
    retained_flags = jnp.where(spike_event[None, :, None], 1.0 - decay_loss, 1.0)
    diagonal = jnp.exp(-rate * spread) * retained_flags
    noise = jnp.clip(jax.random.normal(random_keys[6], (ENERGIES, CHAIN_BLOCKS, ORB, ORB), jnp.float32), -4.0, 4.0)
    noise = noise * (0.15 / jnp.sqrt(jnp.float32(ORB)))
    return noise + jnp.eye(ORB, dtype=jnp.float32) * diagonal[..., None, :]


def draw_mode_shift(key, part):
    shift_keys = jax.random.split(jax.random.fold_in(key, 71), 3)
    covered = jax.random.permutation(shift_keys[0], ENERGIES).astype(jnp.int32)
    extra = jax.random.randint(shift_keys[1], (MODES - ENERGIES,), 0, ENERGIES).astype(jnp.int32)
    joined = jnp.concatenate([covered, extra])
    order = jax.random.permutation(shift_keys[2], MODES)
    return joined[order].astype(jnp.int32)


def levels(rng, shape, shards, low, top_value):
    def one(position, parts):
        heights = jax.random.uniform(jax.random.fold_in(jax.random.fold_in(rng, 6), position), (parts,), jnp.float32, low / len(shards), top_value / len(shards))
        return jnp.repeat(jnp.exp(heights), shape[position] // parts).reshape((-1,) + (1,) * (len(shape) - position - 1))

    gain = one(*shards[0])
    for cut in shards[1:]:
        gain = gain * one(*cut)
    return gain


def scatter_about(stream_key, extent, scale, bound, pieces=(), kind=jnp.bfloat16):
    level = levels(stream_key, extent, pieces, -0.22, 0.18) if pieces else 1.0
    values = jax.random.normal(stream_key, extent, jnp.float32) * scale * level
    return jnp.minimum(jnp.maximum(values, -bound), bound).astype(kind)


def setup_inputs(seed: int = 0) -> dict:
    key_list = jax.random.split(jax.random.key(seed), 6)
    transfer = draw_transfer(jax.random.fold_in(key_list[5], 71), 0)
    source = scatter_about(key_list[1], (ENERGIES, CHAIN_BLOCKS * ORB, COLUMNS), 0.5, 4.0, ((0, 8), (1, 16), (2, 8)), jnp.float32)
    coupling = scatter_about(key_list[2], (ORB, ORB), ORB ** -0.5, 0.25)
    strength = jnp.clip(jnp.exp(jax.random.uniform(key_list[3], (MODES,), jnp.float32, math.log(0.2), math.log(1.0))), 0.2, 1.0)
    mode_shift = draw_mode_shift(jax.random.fold_in(key_list[5], 71), 0)
    return dict(transfer=transfer, source=source, coupling=coupling, strength=strength, mode_shift=mode_shift)


def propagate(mats, srcs):
    def advance(carry, item):
        matrix, piece = item
        fresh = jnp.dot(matrix, carry, precision=lax.Precision.HIGHEST, preferred_element_type=jnp.float32) + piece
        return fresh, fresh

    start = jnp.zeros((ORB, COLUMNS), jnp.float32)
    _, chain_states = lax.scan(advance, start, (mats, srcs))
    return chain_states


def reference(transfer, source, coupling, strength, mode_shift):
    blocks_src = source.reshape(ENERGIES, CHAIN_BLOCKS, ORB, COLUMNS)
    green = lax.map(lambda pair: propagate(pair[0], pair[1]), (transfer, blocks_src))
    density = jnp.mean(green * green, axis=3)
    padded = jnp.pad(density, ((0, 0), (1, 1), (0, 0)))
    smoothed = density + 0.5 * (padded[:, :-2] + padded[:, 2:])
    goal_value = (jnp.arange(ENERGIES, dtype=jnp.int32)[:, None] + mode_shift[None, :]) % ENERGIES
    onehot = (goal_value[:, :, None] == jnp.arange(ENERGIES, dtype=jnp.int32)[None, None, :]).astype(jnp.float32)
    mixing = jnp.sum(strength[None, :, None] * onehot, axis=1)
    selfen = jnp.einsum("ef,fko->eko", mixing, smoothed, precision=lax.Precision.HIGHEST)
    low = green.astype(jnp.bfloat16).astype(jnp.float32)
    wide = coupling.astype(jnp.float32)
    inner = jnp.einsum("oi,ekon->ekin", wide, low)
    scaled = (inner * selfen[..., None]).astype(jnp.bfloat16).astype(jnp.float32)
    scattered = jnp.einsum("io,ekon->ekin", wide, scaled)
    return green.reshape(ENERGIES, CHAIN_BLOCKS * ORB, COLUMNS), scattered.reshape(ENERGIES, CHAIN_BLOCKS * ORB, COLUMNS)
```

```python
import functools

import jax
import jax.numpy as jnp
from jax import lax
from jax.experimental import pallas as pl
from jax.experimental.pallas import tpu as pltpu
from jax.sharding import PartitionSpec as P

MESH = pl.DeviceIdType.MESH
F32, BF16 = jnp.float32, jnp.bfloat16
PIECES = 8
HALVES = 2


def halves(value):
    high = value.astype(BF16)
    return high, (value - high.astype(F32)).astype(BF16)


def nn(left, right):
    return jnp.dot(left, right, preferred_element_type=F32)


def nt(left, right):
    return lax.dot_general(left, right, (((1,), (1,)), ((), ())), preferred_element_type=F32)


def kernel(sizes, t_hbm, s_hbm, coup, w, green, scat, tb, sb, ah, al, bh, bl, t0h, t0l, p1h, p1l, ch, cl, p1, lt, xt, gt, inner,
           gout, sout, part, ga, ed, er, smb, ys, zs, zr, load, store, xs_sem, xr_sem, as_sem, ar_sem, es_sem, er_sem, ys_sem,
           yr_sem, z_sem, up_sem, dn_sem):
    cuts, energies, groups, count = sizes
    ny = energies // HALVES
    nz = HALVES * cuts
    j, e, q = lax.axis_index("cuts"), lax.axis_index("energy"), lax.axis_index("group")
    y = lax.rem(e, ny)
    z = (e // ny) * cuts + j
    orbs, cols = tb.shape[1], xt.shape[0]
    lanes = part.shape[1]
    strips = orbs // lanes
    width = cols // PIECES

    def along_z(step):
        there = lax.rem(z + step + nz, nz)
        return (lax.rem(there, cuts), (there // cuts) * ny + y, q)

    def along_group(step):
        return (j, e, lax.rem(q + step, groups))

    def along_y(step):
        return (j, (e // ny) * ny + lax.rem(y + step, ny), q)

    def local(src, dst, sem):
        return pltpu.make_async_copy(src, dst, sem)

    def remote(src, dst, send, recv, device):
        return pltpu.make_async_remote_copy(src_ref=src, dst_ref=dst, send_sem=send, recv_sem=recv, device_id=device, device_id_type=MESH)

    loads = [local(t_hbm.at[0, k], tb.at[k], load.at[k]) for k in range(count)]
    loads.append(local(s_hbm.at[0], sb, load.at[count]))
    for k in (0, 1, 3, 2):
        loads[k].start()

    barrier = pltpu.get_barrier_semaphore()
    near = [along_z(1), along_z(-1)] + [along_group(r) for r in range(1, groups)] + [along_y(r) for r in range(1, ny)]
    for device in near:
        pl.semaphore_signal(barrier, inc=1, device_id=device, device_id_type=MESH)
    pl.semaphore_wait(barrier, len(near))

    def greet(rnd):
        pl.semaphore_signal(up_sem.at[rnd], inc=1, device_id=along_z(2**rnd), device_id_type=MESH)
        pl.semaphore_signal(dn_sem.at[rnd], inc=1, device_id=along_z(-(2**rnd)), device_id_type=MESH)

    def met(rnd):
        pl.semaphore_wait(up_sem.at[rnd], 1)
        pl.semaphore_wait(dn_sem.at[rnd], 1)

    greet(0)

    loads[0].wait()
    high, low = halves(tb[0].T)
    t0h[...] = high
    t0l[...] = low
    loads[1].wait()
    high, low = halves(tb[1])
    ah[...] = high
    al[...] = low
    met(0)
    greet(1)
    p1[...] = nt(t0h[...], ah[...]) + (nt(t0l[...], ah[...]) + nt(t0h[...], al[...]))
    high, low = halves(p1[...])
    p1h[...] = high
    p1l[...] = low
    loads[3].wait()
    for k in range(count):
        lt[k] = sb[pl.ds(k * orbs, orbs), :].T
    met(1)
    greet(2)
    high, low = halves(lt[0])
    lt[1] = lt[1] + (nt(high, ah[...]) + (nt(low, ah[...]) + nt(high, al[...])))
    loads[2].wait()
    high, low = halves(tb[2])
    bh[...] = high
    bl[...] = low
    high, low = halves(lt[1])
    lt[2] = lt[2] + (nt(high, bh[...]) + (nt(low, bh[...]) + nt(high, bl[...])))

    def piece(p):
        rows = pl.ds(pl.multiple_of(p * width, width), width)
        return rows, remote(gt.at[2, rows], xt.at[rows], xs_sem.at[p], xr_sem.at[p], along_z(1))

    @pl.when(j == 0)
    def _():
        for k in range(count):
            gt[k] = lt[k]

        def send(p, _):
            piece(p)[1].start()
            return 0

        lax.fori_loop(0, PIECES, send, 0)

    p1[...] = nt(p1h[...], bh[...]) + (nt(p1l[...], bh[...]) + nt(p1h[...], bl[...]))
    high, low = halves(p1[...])
    ch[...] = high
    cl[...] = low
    met(2)
    greet(3)

    @pl.when(j > 0)
    def _():
        def pass_on(p, _):
            rows, copy = piece(p)
            copy.wait_recv()
            incoming = xt[rows, :]
            rest = incoming - incoming.astype(BF16).astype(F32)
            both = jnp.concatenate([incoming, rest], axis=0).astype(BF16)
            product = nn(both, ch[...]) + nn(both, cl[...])
            gt[2, rows] = lt[2, rows] + (product[:width] + product[width:])

            @pl.when(j < cuts - 1)
            def _():
                copy.start()

            return 0

        lax.fori_loop(0, PIECES, pass_on, 0)
        high, low = halves(xt[...])
        gt[0] = lt[0] + (nn(high, t0h[...]) + (nn(low, t0h[...]) + nn(high, t0l[...])))
        gt[1] = lt[1] + (nn(high, p1h[...]) + (nn(low, p1h[...]) + nn(high, p1l[...])))

    part[...] = jnp.zeros_like(part)
    for k in range(count):
        square = gt[k] * gt[k]
        total = jnp.sum(square, axis=0, keepdims=True)
        for i in range(strips):
            part[k * strips + i : k * strips + i + 1, :] = total[:, i * lanes : (i + 1) * lanes]
    sums = [remote(part, ga.at[r - 1], as_sem.at[r - 1], ar_sem.at[r - 1], along_group(r)) for r in range(1, groups)]
    for copy in sums:
        copy.start()
    for k in range(count):
        inner[k] = nn(gt[k].astype(BF16), coup[...])
    for copy in sums:
        copy.wait_recv()
    whole = part[...]
    for r in range(1, groups):
        whole = whole + ga[r - 1]
    n = count * strips
    ed[0] = whole[0:8]
    ed[1] = whole[n - 8 : n]
    down = remote(ed.at[0], er.at[1], es_sem.at[0], er_sem.at[1], along_z(-1))
    rise = remote(ed.at[1], er.at[0], es_sem.at[1], er_sem.at[0], along_z(1))

    @pl.when(j > 0)
    def _():
        down.start()

    @pl.when(j < cuts - 1)
    def _():
        rise.start()

    @pl.when(j == 0)
    def _():
        er[0] = jnp.zeros_like(er[0])

    @pl.when(j == cuts - 1)
    def _():
        er[1] = jnp.zeros_like(er[1])

    @pl.when(j > 0)
    def _():
        rise.wait_recv()

    @pl.when(j < cuts - 1)
    def _():
        down.wait_recv()

    left = jnp.concatenate([er[0, 8 - strips : 8], whole[0 : n - strips]], axis=0)
    right = jnp.concatenate([whole[strips:n], er[1, 0:strips]], axis=0)
    smb[...] = jnp.zeros_like(smb)
    smb[0:n] = whole[0:n] + 0.5 * (left + right)
    smooth = [remote(smb, ys.at[r - 1], ys_sem.at[r - 1], yr_sem.at[r - 1], along_y(r)) for r in range(1, ny)]
    for copy in smooth:
        copy.start()
    own = smb[...] * w[0:1, :]
    other = smb[...] * w[ny : ny + 1, :]
    for r in range(1, ny):
        smooth[r - 1].wait_recv()
        own = own + ys[r - 1] * w[r : r + 1, :]
        other = other + ys[r - 1] * w[ny + r : ny + r + 1, :]
    zs[...] = other
    met(3)
    across = remote(zs, zr, z_sem.at[0], z_sem.at[1], along_z(cuts))
    across.start()
    for k in range(count):
        gout[pl.ds(k * orbs, orbs), :] = gt[k].T
    stores = [local(gout, green.at[0], store.at[0])]
    stores[0].start()
    across.wait_recv()
    selfen = own + zr[...]
    for k in range(count):
        row = jnp.concatenate([selfen[k * strips + i : k * strips + i + 1, :] for i in range(strips)], axis=1)
        scaled = (inner[k] * row).astype(BF16)
        rows = pl.ds(k * orbs, orbs)
        sout[rows, :] = nt(coup[...], scaled)
        copy = local(sout.at[rows], scat.at[0, rows], store.at[k + 1])
        copy.start()
        stores.append(copy)

    @pl.when(j < cuts - 1)
    def _():
        def sent(p, _):
            piece(p)[1].wait_send()
            return 0

        lax.fori_loop(0, PIECES, sent, 0)
        rise.wait_send()

    @pl.when(j > 0)
    def _():
        down.wait_send()

    for copy in sums + smooth + [across]:
        copy.wait_send()
    for copy in stores:
        copy.wait()


def body(sizes, transfer, source, coupling, strength, mode_shift):
    cuts, energies, groups = sizes
    count, orbs = transfer.shape[1], transfer.shape[2]
    rows, cols = source.shape[1], source.shape[2]
    ny = energies // HALVES
    e = lax.axis_index("energy")
    y, half = e % ny, e // ny
    targets = jnp.stack([e, (e + ny) % energies])
    froms = half * ny + (y - jnp.arange(ny, dtype=jnp.int32)) % ny
    goal = (targets[:, None] + mode_shift[None, :]) % energies
    hits = goal[:, None, :] == froms[None, :, None]
    weights = jnp.sum(jnp.where(hits, strength[None, None, :], 0.0), axis=2) / (cols * groups)
    lanes = 128
    weights = jnp.broadcast_to(weights.reshape(2 * ny, 1), (2 * ny, lanes))
    vmem = pltpu.VMEM
    dma = pltpu.SemaphoreType.DMA
    small = 16
    any_space = pl.BlockSpec(memory_space=pl.ANY)
    in_vmem = pl.BlockSpec(memory_space=pltpu.VMEM)
    out = jax.ShapeDtypeStruct(source.shape, F32)
    return pl.pallas_call(
        functools.partial(kernel, (cuts, energies, groups, count)),
        out_shape=(out, out),
        in_specs=[any_space, any_space, in_vmem, in_vmem],
        out_specs=(any_space, any_space),
        scratch_shapes=[
            vmem((count, orbs, orbs), F32),
            vmem((rows, cols), F32),
            *[vmem((orbs, orbs), BF16) for _ in range(10)],
            vmem((orbs, orbs), F32),
            vmem((count, cols, orbs), F32),
            vmem((cols, orbs), F32),
            vmem((count, cols, orbs), F32),
            vmem((count, cols, orbs), F32),
            vmem((rows, cols), F32),
            vmem((rows, cols), F32),
            vmem((small, lanes), F32),
            vmem((groups - 1, small, lanes), F32),
            vmem((2, 8, lanes), F32),
            vmem((2, 8, lanes), F32),
            vmem((small, lanes), F32),
            vmem((ny - 1, small, lanes), F32),
            vmem((small, lanes), F32),
            vmem((small, lanes), F32),
            dma((count + 1,)),
            dma((count + 1,)),
            dma((PIECES,)),
            dma((PIECES,)),
            dma((groups - 1,)),
            dma((groups - 1,)),
            dma((2,)),
            dma((2,)),
            dma((ny - 1,)),
            dma((ny - 1,)),
            dma((2,)),
            pltpu.SemaphoreType.REGULAR((4,)),
            pltpu.SemaphoreType.REGULAR((4,)),
        ],
        compiler_params=pltpu.CompilerParams(collective_id=0, has_side_effects=True, vmem_limit_bytes=48 * 2**20),
        name="propagate_scatter",
    )(transfer, source, coupling, weights)


def solution(mesh):
    sizes = tuple(mesh.shape[name] for name in ("cuts", "energy", "group"))
    in_specs = (P("energy", "cuts", None, None), P("energy", "cuts", "group"), P(), P(), P())
    out_specs = (P("energy", "cuts", "group"), P("energy", "cuts", "group"))
    return jax.shard_map(functools.partial(body, sizes), mesh=mesh, in_specs=in_specs, out_specs=out_specs, check_vma=False)
```

```python
import functools

import jax
import jax.numpy as jnp
from jax import lax
from jax.experimental import pallas as pl
from jax.experimental.pallas import tpu as pltpu
from jax.sharding import PartitionSpec as P

MESH = pl.DeviceIdType.MESH
F32, BF16 = jnp.float32, jnp.bfloat16
PIECES = 16
HALVES = 2


def halves(value):
    high = value.astype(BF16)
    return high, (value - high.astype(F32)).astype(BF16)


def nn(left, right):
    return jnp.dot(left, right, preferred_element_type=F32)


def nt(left, right):
    return lax.dot_general(left, right, (((1,), (1,)), ((), ())), preferred_element_type=F32)


def kernel(sizes, t_hbm, s_hbm, c_hbm, strength, shift, gout, inner, sel, coup, tb, sb, ah, al, bh, bl, t0h, t0l, p1h, p1l, ch, cl,
           p1, lt, xt, gt, part, ga, ys, zs, zr, eds, edr, load, xs_sem, xr_sem, as_sem, ar_sem, ys_sem, yr_sem, z_sem, es_sem, er_sem,
           up_sem, dn_sem):
    cuts, energies, groups, count = sizes
    ny = energies // HALVES
    nz = HALVES * cuts
    j, e, q = lax.axis_index("cuts"), lax.axis_index("energy"), lax.axis_index("group")
    y = lax.rem(e, ny)
    z = (e // ny) * cuts + j
    orbs, cols = tb.shape[1], xt.shape[0]
    lanes = part.shape[1]
    strips = orbs // lanes
    width = cols // PIECES

    def along_z(step):
        there = lax.rem(z + step + nz, nz)
        return (lax.rem(there, cuts), (there // cuts) * ny + y, q)

    def along_group(step):
        return (j, e, lax.rem(q + step, groups))

    def along_y(step):
        return (j, (e // ny) * ny + lax.rem(y + step, ny), q)

    def local(src, dst, sem):
        return pltpu.make_async_copy(src, dst, sem)

    def remote(src, dst, send, recv, device):
        return pltpu.make_async_remote_copy(src_ref=src, dst_ref=dst, send_sem=send, recv_sem=recv, device_id=device, device_id_type=MESH)

    loads = [local(t_hbm.at[0, k], tb.at[k], load.at[k]) for k in range(count)]
    loads.append(local(s_hbm.at[0], sb, load.at[count]))
    loads.append(local(c_hbm, coup, load.at[count + 1]))
    for k in (count, *range(1, count), 0, count + 1):
        loads[k].start()

    barrier = pltpu.get_barrier_semaphore()
    near = [along_z(1), along_z(-1)] + [along_group(r) for r in range(1, groups)] + [along_y(r) for r in range(1, ny)]
    for device in near:
        pl.semaphore_signal(barrier, inc=1, device_id=device, device_id_type=MESH)
    pl.semaphore_wait(barrier, len(near))

    def greet(rnd):
        pl.semaphore_signal(up_sem.at[rnd], inc=1, device_id=along_z(2**rnd), device_id_type=MESH)
        pl.semaphore_signal(dn_sem.at[rnd], inc=1, device_id=along_z(-(2**rnd)), device_id_type=MESH)

    def met(rnd):
        pl.semaphore_wait(up_sem.at[rnd], 1)
        pl.semaphore_wait(dn_sem.at[rnd], 1)

    greet(0)

    def weight(target, source):
        total = 0.0
        for m in range(strength.shape[0]):
            total = total + jnp.where(lax.rem(target + shift[m], energies) == source, strength[m], 0.0)
        return total / (cols * groups)

    sources = [(e // ny) * ny + lax.rem(y - r + ny, ny) for r in range(ny)]
    w = [[weight(target, source) for source in sources] for target in (e, lax.rem(e + ny, energies))]

    loads[count].wait()
    for k in range(count):
        lt[k] = sb[pl.ds(k * orbs, orbs), :].T
    loads[1].wait()
    ah[...], al[...] = halves(tb[1])
    high, low = halves(lt[0])
    lt[1] = lt[1] + (nt(high, ah[...]) + (nt(low, ah[...]) + nt(high, al[...])))
    loads[2].wait()
    bh[...], bl[...] = halves(tb[2])
    high, low = halves(lt[1])
    lt[2] = lt[2] + (nt(high, bh[...]) + (nt(low, bh[...]) + nt(high, bl[...])))

    def piece(p):
        rows = pl.ds(pl.multiple_of(p * width, width), width)
        return rows, remote(gt.at[2, rows], xt.at[rows], xs_sem.at[p], xr_sem.at[p], along_z(1))

    @pl.when(j == 0)
    def _():
        gt[2] = lt[2]

        def send(p, _):
            piece(p)[1].start()
            return 0

        lax.fori_loop(0, PIECES, send, 0)
        gt[0] = lt[0]
        gt[1] = lt[1]

    met(0)
    greet(1)

    loads[0].wait()
    t0h[...], t0l[...] = halves(tb[0].T)
    p1[...] = nt(t0h[...], ah[...]) + (nt(t0l[...], ah[...]) + nt(t0h[...], al[...]))
    p1h[...], p1l[...] = halves(p1[...])
    met(1)
    greet(2)
    p1[...] = nt(p1h[...], bh[...]) + (nt(p1l[...], bh[...]) + nt(p1h[...], bl[...]))
    ch[...], cl[...] = halves(p1[...])
    met(2)
    greet(3)
    loads[count + 1].wait()

    @pl.when(j > 0)
    def _():
        def pass_on(p, _):
            rows, copy = piece(p)
            copy.wait_recv()
            incoming = xt[rows, :]
            rest = incoming - incoming.astype(BF16).astype(F32)
            both = jnp.concatenate([incoming, rest], axis=0).astype(BF16)
            product = nn(both, ch[...]) + nn(both, cl[...])
            gt[2, rows] = lt[2, rows] + (product[:width] + product[width:])

            @pl.when(j < cuts - 1)
            def _():
                copy.start()

            return 0

        lax.fori_loop(0, PIECES, pass_on, 0)
        high, low = halves(xt[...])
        gt[0] = lt[0] + (nn(high, t0h[...]) + (nn(low, t0h[...]) + nn(high, t0l[...])))
        gt[1] = lt[1] + (nn(high, p1h[...]) + (nn(low, p1h[...]) + nn(high, p1l[...])))

    part[...] = jnp.zeros_like(part)
    for k in range(count):
        square = gt[k] * gt[k]
        total = jnp.sum(square, axis=0, keepdims=True)
        for i in range(strips):
            part[k * strips + i : k * strips + i + 1, :] = total[:, i * lanes : (i + 1) * lanes]
    sums = [remote(part, ga.at[r - 1], as_sem.at[r - 1], ar_sem.at[r - 1], along_group(r)) for r in range(1, groups)]
    for copy in sums:
        copy.start()
    for k in range(count):
        inner[k] = nn(gt[k].astype(BF16), coup[...])
    for copy in sums:
        copy.wait_recv()
    whole = part[...]
    for r in range(1, groups):
        whole = whole + ga[r - 1]
    zs[2] = whole
    dense = [remote(zs.at[2], ys.at[r - 1], ys_sem.at[r - 1], yr_sem.at[r - 1], along_y(r)) for r in range(1, ny)]
    for copy in dense:
        copy.start()
    own = whole * w[0][0]
    other = whole * w[1][0]
    for k in range(count):
        gout[pl.ds(k * orbs, orbs), :] = gt[k].T
    for r in range(1, ny):
        dense[r - 1].wait_recv()
        own = own + ys[r - 1] * w[0][r]
        other = other + ys[r - 1] * w[1][r]
    n = count * strips
    zs[0] = other
    for t, value in enumerate((own, other)):
        eds[t, 0] = value[0:8]
        eds[t, 1] = value[n - 8 : n]
    met(3)
    across = remote(zs.at[0], zr, z_sem.at[0], z_sem.at[1], along_z(cuts))
    across.start()
    down = [remote(eds.at[t, 0], edr.at[t, 1], es_sem.at[t, 0], er_sem.at[t, 1], along_z(t * cuts - 1)) for t in (1, 0)]
    rise = [remote(eds.at[t, 1], edr.at[t, 0], es_sem.at[t, 1], er_sem.at[t, 0], along_z(t * cuts + 1)) for t in (1, 0)]

    @pl.when(j > 0)
    def _():
        for copy in down:
            copy.start()

    @pl.when(j < cuts - 1)
    def _():
        for copy in rise:
            copy.start()

    @pl.when(j == 0)
    def _():
        for t in (0, 1):
            edr[t, 0] = jnp.zeros_like(edr[t, 0])

    @pl.when(j == cuts - 1)
    def _():
        for t in (0, 1):
            edr[t, 1] = jnp.zeros_like(edr[t, 1])

    @pl.when(j > 0)
    def _():
        for copy in rise:
            copy.wait_recv()

    @pl.when(j < cuts - 1)
    def _():
        for copy in down:
            copy.wait_recv()

    across.wait_recv()
    total = own + zr[...]
    left = jnp.concatenate([edr[0, 0, 8 - strips : 8] + edr[1, 0, 8 - strips : 8], total[0 : n - strips]], axis=0)
    right = jnp.concatenate([total[strips:n], edr[0, 1, 0:strips] + edr[1, 1, 0:strips]], axis=0)
    sel[0:n] = total[0:n] + 0.5 * (left + right)

    @pl.when(j < cuts - 1)
    def _():
        def sent(p, _):
            piece(p)[1].wait_send()
            return 0

        lax.fori_loop(0, PIECES, sent, 0)
        for copy in rise:
            copy.wait_send()

    @pl.when(j > 0)
    def _():
        for copy in down:
            copy.wait_send()

    for copy in sums + dense + [across]:
        copy.wait_send()


def finish(gin, inner, sel, c_hbm, green, scat, coup, sout, sem):
    count, orbs, lanes = inner.shape[0], inner.shape[2], sel.shape[1]
    strips = orbs // lanes
    stores = [pltpu.make_async_copy(gin, green.at[0], sem.at[count])]
    stores[0].start()
    fetch = pltpu.make_async_copy(c_hbm, coup, sem.at[count + 1])
    fetch.start()
    fetch.wait()
    for k in range(count):
        row = jnp.concatenate([sel[k * strips + i : k * strips + i + 1, :] for i in range(strips)], axis=1)
        rows = pl.ds(k * orbs, orbs)
        sout[rows, :] = nt(coup[...], (inner[k] * row).astype(BF16))
        stores.append(pltpu.make_async_copy(sout.at[rows], scat.at[0, rows], sem.at[k]))
        stores[-1].start()
    for copy in stores:
        copy.wait()


def body(sizes, transfer, source, coupling, strength, mode_shift):
    cuts, energies, groups = sizes
    count, orbs = transfer.shape[1], transfer.shape[2]
    rows, cols = source.shape[1], source.shape[2]
    ny = energies // HALVES
    lanes = 128
    vmem = pltpu.VMEM
    dma = pltpu.SemaphoreType.DMA
    small = 16
    hbm = pl.BlockSpec(memory_space=pltpu.HBM)
    in_vmem = pl.BlockSpec(memory_space=pltpu.VMEM)
    scalars = pl.BlockSpec(memory_space=pltpu.SMEM)
    struct = jax.ShapeDtypeStruct
    coupled = [vmem((orbs, orbs), BF16)]
    green, inner, sel = pl.pallas_call(
        functools.partial(kernel, (cuts, energies, groups, count)),
        out_shape=(struct((rows, cols), F32), struct((count, cols, orbs), F32), struct((small, lanes), F32)),
        in_specs=[hbm, hbm, hbm, scalars, scalars],
        out_specs=(in_vmem, in_vmem, in_vmem),
        scratch_shapes=[
            *coupled,
            vmem((count, orbs, orbs), F32),
            vmem((rows, cols), F32),
            *[vmem((orbs, orbs), BF16) for _ in range(10)],
            vmem((orbs, orbs), F32),
            vmem((count, cols, orbs), F32),
            vmem((cols, orbs), F32),
            vmem((count, cols, orbs), F32),
            vmem((small, lanes), F32),
            vmem((groups - 1, small, lanes), F32),
            vmem((ny - 1, small, lanes), F32),
            vmem((3, small, lanes), F32),
            vmem((small, lanes), F32),
            vmem((2, 2, 8, lanes), F32),
            vmem((2, 2, 8, lanes), F32),
            dma((count + 2,)),
            dma((PIECES,)),
            dma((PIECES,)),
            dma((groups - 1,)),
            dma((groups - 1,)),
            dma((ny - 1,)),
            dma((ny - 1,)),
            dma((2,)),
            dma((2, 2)),
            dma((2, 2)),
            pltpu.SemaphoreType.REGULAR((4,)),
            pltpu.SemaphoreType.REGULAR((4,)),
        ],
        compiler_params=pltpu.CompilerParams(collective_id=0, has_side_effects=True, vmem_limit_bytes=54000000),
        name="propagate",
    )(transfer, source, coupling, strength, mode_shift)
    out = struct(source.shape, F32)
    return pl.pallas_call(
        finish,
        out_shape=(out, out),
        in_specs=[in_vmem, in_vmem, in_vmem, hbm],
        out_specs=(hbm, hbm),
        scratch_shapes=[*coupled, vmem((rows, cols), F32), dma((count + 2,))],
        compiler_params=pltpu.CompilerParams(vmem_limit_bytes=16 * 2**20),
        name="finish",
    )(green, inner, sel, coupling)


def solution(mesh):
    sizes = tuple(mesh.shape[name] for name in ("cuts", "energy", "group"))
    in_specs = (P("energy", "cuts", None, None), P("energy", "cuts", "group"), P(), P(), P())
    out_specs = (P("energy", "cuts", "group"), P("energy", "cuts", "group"))
    return jax.shard_map(functools.partial(body, sizes), mesh=mesh, in_specs=in_specs, out_specs=out_specs, check_vma=False)
```

```python
import functools

import jax
import jax.numpy as jnp
from jax import lax
from jax.experimental import pallas as pl
from jax.experimental.pallas import tpu as pltpu
from jax.sharding import PartitionSpec as P

MESH = pl.DeviceIdType.MESH
F32, BF16 = jnp.float32, jnp.bfloat16
PIECES = 16
HALVES = 2


def halves(value):
    high = value.astype(BF16)
    return high, (value - high.astype(F32)).astype(BF16)


def nn(left, right):
    return jnp.dot(left, right, preferred_element_type=F32)


def nt(left, right):
    return lax.dot_general(left, right, (((1,), (1,)), ((), ())), preferred_element_type=F32)


def kernel(sizes, t_hbm, s_hbm, c_hbm, strength_hbm, shift_hbm, gout, inner, sel, strength, shift, coup, tb, sb, ah, al, bh, bl, t0h, t0l, p1h, p1l, ch, cl,
           p1, lt, xt, gt, part, ga, ys, zs, zr, eds, edr, load, xs_sem, xr_sem, as_sem, ar_sem, ys_sem, yr_sem, z_sem, es_sem, er_sem,
           up_sem, dn_sem):
    cuts, energies, groups, count = sizes
    ny = energies // HALVES
    nz = HALVES * cuts
    j, e, q = lax.axis_index("cuts"), lax.axis_index("energy"), lax.axis_index("group")
    y = lax.rem(e, ny)
    z = (e // ny) * cuts + j
    orbs, cols = tb.shape[1], xt.shape[0]
    lanes = part.shape[1]
    strips = orbs // lanes
    width = cols // PIECES

    def along_z(step):
        there = lax.rem(z + step + nz, nz)
        return (lax.rem(there, cuts), (there // cuts) * ny + y, q)

    def along_group(step):
        return (j, e, lax.rem(q + step, groups))

    def along_y(step):
        return (j, (e // ny) * ny + lax.rem(y + step, ny), q)

    def local(src, dst, sem):
        return pltpu.make_async_copy(src, dst, sem)

    def remote(src, dst, send, recv, device):
        return pltpu.make_async_remote_copy(src_ref=src, dst_ref=dst, send_sem=send, recv_sem=recv, device_id=device, device_id_type=MESH)

    loads = [local(t_hbm.at[0, k], tb.at[k], load.at[k]) for k in range(count)]
    loads.append(local(s_hbm.at[0], sb, load.at[count]))
    loads.append(local(c_hbm, coup, load.at[count + 1]))
    loads.append(local(strength_hbm, strength, load.at[count + 2]))
    loads.append(local(shift_hbm, shift, load.at[count + 3]))
    for k in (count, *range(1, count), 0, count + 1, count + 2, count + 3):
        loads[k].start()

    barrier = pltpu.get_barrier_semaphore()
    near = [along_z(1), along_z(-1)] + [along_group(r) for r in range(1, groups)] + [along_y(r) for r in range(1, ny)]
    for device in near:
        pl.semaphore_signal(barrier, inc=1, device_id=device, device_id_type=MESH)
    pl.semaphore_wait(barrier, len(near))

    def greet(rnd):
        pl.semaphore_signal(up_sem.at[rnd], inc=1, device_id=along_z(2**rnd), device_id_type=MESH)
        pl.semaphore_signal(dn_sem.at[rnd], inc=1, device_id=along_z(-(2**rnd)), device_id_type=MESH)

    def met(rnd):
        pl.semaphore_wait(up_sem.at[rnd], 1)
        pl.semaphore_wait(dn_sem.at[rnd], 1)

    greet(0)

    loads[count].wait()
    for k in range(count):
        lt[k] = sb[pl.ds(k * orbs, orbs), :].T
    loads[1].wait()
    ah[...], al[...] = halves(tb[1])
    high, low = halves(lt[0])
    lt[1] = lt[1] + (nt(high, ah[...]) + (nt(low, ah[...]) + nt(high, al[...])))
    loads[2].wait()
    bh[...], bl[...] = halves(tb[2])
    high, low = halves(lt[1])
    lt[2] = lt[2] + (nt(high, bh[...]) + (nt(low, bh[...]) + nt(high, bl[...])))

    def piece(p):
        rows = pl.ds(pl.multiple_of(p * width, width), width)
        return rows, remote(gt.at[2, rows], xt.at[rows], xs_sem.at[p], xr_sem.at[p], along_z(1))

    @pl.when(j == 0)
    def _():
        gt[2] = lt[2]

        def send(p, _):
            piece(p)[1].start()
            return 0

        lax.fori_loop(0, PIECES, send, 0)
        gt[0] = lt[0]
        gt[1] = lt[1]

    met(0)
    greet(1)

    loads[0].wait()
    t0h[...], t0l[...] = halves(tb[0].T)
    p1[...] = nt(t0h[...], ah[...]) + (nt(t0l[...], ah[...]) + nt(t0h[...], al[...]))
    p1h[...], p1l[...] = halves(p1[...])
    met(1)
    greet(2)
    p1[...] = nt(p1h[...], bh[...]) + (nt(p1l[...], bh[...]) + nt(p1h[...], bl[...]))
    ch[...], cl[...] = halves(p1[...])
    @pl.when(j >= 4)
    def _():
        met(2)
        greet(3)

    loads[count + 1].wait()

    @pl.when(j > 0)
    def _():
        def pass_on(p, _):
            rows, copy = piece(p)
            copy.wait_recv()
            incoming = xt[rows, :]
            rest = incoming - incoming.astype(BF16).astype(F32)
            both = jnp.concatenate([incoming, rest], axis=0).astype(BF16)
            product = nn(both, ch[...]) + nn(both, cl[...])
            gt[2, rows] = lt[2, rows] + (product[:width] + product[width:])

            @pl.when(j < cuts - 1)
            def _():
                copy.start()

            return 0

        lax.fori_loop(0, PIECES, pass_on, 0)
        high, low = halves(xt[...])
        gt[0] = lt[0] + (nn(high, t0h[...]) + (nn(low, t0h[...]) + nn(high, t0l[...])))
        gt[1] = lt[1] + (nn(high, p1h[...]) + (nn(low, p1h[...]) + nn(high, p1l[...])))

    @pl.when(j < 4)
    def _():
        met(2)
        greet(3)

    part[...] = jnp.zeros_like(part)
    for k in range(count):
        square = gt[k] * gt[k]
        total = jnp.sum(square, axis=0, keepdims=True)
        for i in range(strips):
            part[k * strips + i : k * strips + i + 1, :] = total[:, i * lanes : (i + 1) * lanes]
    sums = [remote(part, ga.at[r - 1], as_sem.at[r - 1], ar_sem.at[r - 1], along_group(r)) for r in range(1, groups)]
    for copy in sums:
        copy.start()
    for k in range(count):
        inner[k] = nn(gt[k].astype(BF16), coup[...])
    loads[count + 2].wait()
    loads[count + 3].wait()

    def weight(target, source):
        total = 0.0
        for m in range(strength.shape[0]):
            total = total + jnp.where(lax.rem(target + shift[m], energies) == source, strength[m], 0.0)
        return total / (cols * groups)

    sources = [(e // ny) * ny + lax.rem(y - r + ny, ny) for r in range(ny)]
    w = [[weight(target, source) for source in sources] for target in (e, lax.rem(e + ny, energies))]

    for copy in sums:
        copy.wait_recv()
    whole = part[...]
    for r in range(1, groups):
        whole = whole + ga[r - 1]
    zs[2] = whole
    dense = [remote(zs.at[2], ys.at[r - 1], ys_sem.at[r - 1], yr_sem.at[r - 1], along_y(r)) for r in range(1, ny)]
    for copy in dense:
        copy.start()
    own = whole * w[0][0]
    other = whole * w[1][0]
    for k in range(count):
        gout[pl.ds(k * orbs, orbs), :] = gt[k].T
    for r in range(1, ny):
        dense[r - 1].wait_recv()
        own = own + ys[r - 1] * w[0][r]
        other = other + ys[r - 1] * w[1][r]
    n = count * strips
    zs[0] = other
    for t, value in enumerate((own, other)):
        eds[t, 0] = value[0:8]
        eds[t, 1] = value[n - 8 : n]
    met(3)
    across = remote(zs.at[0], zr, z_sem.at[0], z_sem.at[1], along_z(cuts))
    across.start()
    down = [remote(eds.at[t, 0], edr.at[t, 1], es_sem.at[t, 0], er_sem.at[t, 1], along_z(t * cuts - 1)) for t in (1, 0)]
    rise = [remote(eds.at[t, 1], edr.at[t, 0], es_sem.at[t, 1], er_sem.at[t, 0], along_z(t * cuts + 1)) for t in (1, 0)]

    @pl.when(j > 0)
    def _():
        for copy in down:
            copy.start()

    @pl.when(j < cuts - 1)
    def _():
        for copy in rise:
            copy.start()

    @pl.when(j == 0)
    def _():
        for t in (0, 1):
            edr[t, 0] = jnp.zeros_like(edr[t, 0])

    @pl.when(j == cuts - 1)
    def _():
        for t in (0, 1):
            edr[t, 1] = jnp.zeros_like(edr[t, 1])

    @pl.when(j > 0)
    def _():
        for copy in rise:
            copy.wait_recv()

    @pl.when(j < cuts - 1)
    def _():
        for copy in down:
            copy.wait_recv()

    across.wait_recv()
    total = own + zr[...]
    left = jnp.concatenate([edr[0, 0, 8 - strips : 8] + edr[1, 0, 8 - strips : 8], total[0 : n - strips]], axis=0)
    right = jnp.concatenate([total[strips:n], edr[0, 1, 0:strips] + edr[1, 1, 0:strips]], axis=0)
    sel[0:n] = total[0:n] + 0.5 * (left + right)

    @pl.when(j < cuts - 1)
    def _():
        def sent(p, _):
            piece(p)[1].wait_send()
            return 0

        lax.fori_loop(0, PIECES, sent, 0)
        for copy in rise:
            copy.wait_send()

    @pl.when(j > 0)
    def _():
        for copy in down:
            copy.wait_send()

    for copy in sums + dense + [across]:
        copy.wait_send()


def finish(gin, inner, sel, c_hbm, green, scat, coup, sout, sem):
    count, orbs, lanes = inner.shape[0], inner.shape[2], sel.shape[1]
    strips = orbs // lanes
    stores = [pltpu.make_async_copy(gin, green.at[0], sem.at[count])]
    stores[0].start()
    fetch = pltpu.make_async_copy(c_hbm, coup, sem.at[count + 1])
    fetch.start()
    fetch.wait()
    for k in range(count):
        row = jnp.concatenate([sel[k * strips + i : k * strips + i + 1, :] for i in range(strips)], axis=1)
        rows = pl.ds(k * orbs, orbs)
        sout[rows, :] = nt(coup[...], (inner[k] * row).astype(BF16))
        stores.append(pltpu.make_async_copy(sout.at[rows], scat.at[0, rows], sem.at[k]))
        stores[-1].start()
    for copy in stores:
        copy.wait()


def body(sizes, transfer, source, coupling, strength, mode_shift):
    cuts, energies, groups = sizes
    count, orbs = transfer.shape[1], transfer.shape[2]
    rows, cols = source.shape[1], source.shape[2]
    ny = energies // HALVES
    lanes = 128
    vmem = pltpu.VMEM
    dma = pltpu.SemaphoreType.DMA
    small = 16
    hbm = pl.BlockSpec(memory_space=pltpu.HBM)
    in_vmem = pl.BlockSpec(memory_space=pltpu.VMEM)
    struct = jax.ShapeDtypeStruct
    coupled = [vmem((orbs, orbs), BF16)]
    green, inner, sel = pl.pallas_call(
        functools.partial(kernel, (cuts, energies, groups, count)),
        out_shape=(struct((rows, cols), F32), struct((count, cols, orbs), F32), struct((small, lanes), F32)),
        in_specs=[hbm] * 5,
        out_specs=(in_vmem, in_vmem, in_vmem),
        scratch_shapes=[
            pltpu.SMEM(strength.shape, F32),
            pltpu.SMEM(mode_shift.shape, jnp.int32),
            *coupled,
            vmem((count, orbs, orbs), F32),
            vmem((rows, cols), F32),
            *[vmem((orbs, orbs), BF16) for _ in range(10)],
            vmem((orbs, orbs), F32),
            vmem((count, cols, orbs), F32),
            vmem((cols, orbs), F32),
            vmem((count, cols, orbs), F32),
            vmem((small, lanes), F32),
            vmem((groups - 1, small, lanes), F32),
            vmem((ny - 1, small, lanes), F32),
            vmem((3, small, lanes), F32),
            vmem((small, lanes), F32),
            vmem((2, 2, 8, lanes), F32),
            vmem((2, 2, 8, lanes), F32),
            dma((count + 4,)),
            dma((PIECES,)),
            dma((PIECES,)),
            dma((groups - 1,)),
            dma((groups - 1,)),
            dma((ny - 1,)),
            dma((ny - 1,)),
            dma((2,)),
            dma((2, 2)),
            dma((2, 2)),
            pltpu.SemaphoreType.REGULAR((4,)),
            pltpu.SemaphoreType.REGULAR((4,)),
        ],
        compiler_params=pltpu.CompilerParams(collective_id=0, has_side_effects=True, vmem_limit_bytes=54000000),
        name="propagate",
    )(*[pltpu.with_memory_space_constraint(a, pltpu.HBM) for a in (transfer, source, coupling, strength, mode_shift)])
    out = struct(source.shape, F32)
    return pl.pallas_call(
        finish,
        out_shape=(out, out),
        in_specs=[in_vmem, in_vmem, in_vmem, hbm],
        out_specs=(hbm, hbm),
        scratch_shapes=[*coupled, vmem((rows, cols), F32), dma((count + 2,))],
        compiler_params=pltpu.CompilerParams(vmem_limit_bytes=16 * 2**20),
        name="finish",
    )(green, inner, sel, coupling)


def solution(mesh):
    sizes = tuple(mesh.shape[name] for name in ("cuts", "energy", "group"))
    in_specs = (P("energy", "cuts", None, None), P("energy", "cuts", "group"), P(), P(), P())
    out_specs = (P("energy", "cuts", "group"), P("energy", "cuts", "group"))
    return jax.shard_map(functools.partial(body, sizes), mesh=mesh, in_specs=in_specs, out_specs=out_specs, check_vma=False)
```

```python
import functools

import jax
import jax.numpy as jnp
from jax import lax
from jax.experimental import pallas as pl
from jax.experimental.pallas import tpu as pltpu
from jax.sharding import PartitionSpec as P

MESH = pl.DeviceIdType.MESH
F32, BF16 = jnp.float32, jnp.bfloat16
PIECES = 16
HALVES = 2
FIRST = 7


def halves(value):
    high = value.astype(BF16)
    return high, (value - high.astype(F32)).astype(BF16)


def nn(left, right):
    return jnp.dot(left, right, preferred_element_type=F32)


def nt(left, right):
    return lax.dot_general(left, right, (((1,), (1,)), ((), ())), preferred_element_type=F32)


def kernel(sizes, t_hbm, s_hbm, c_hbm, strength_hbm, shift_hbm, gout, inner, sel, strength, shift, coup, tb, sb, ah, al, bh, bl, t0h, t0l, p1h, p1l, ch, cl,
           p1, cin, cih, cil, oin, lt, xt, gt, part, ga, ys, zs, zr, eds, edr, load, xs_sem, xr_sem, as_sem, ar_sem, ys_sem, yr_sem, z_sem, es_sem, er_sem,
           cs_sem, cr_sem, ps_sem, pr_sem, ls_sem, up_sem, dn_sem):
    cuts, energies, groups, count = sizes
    ny = energies // HALVES
    nz = HALVES * cuts
    j, e, q = lax.axis_index("cuts"), lax.axis_index("energy"), lax.axis_index("group")
    y = lax.rem(e, ny)
    z = (e // ny) * cuts + j
    orbs, cols = tb.shape[1], xt.shape[0]
    lanes = part.shape[1]
    strips = orbs // lanes
    width = cols // PIECES
    core = lax.rem(q, 2)
    odd = lax.rem(j, 2)
    skips = (odd == 1) & (j >= FIRST) & (j < cuts - 4)
    fed = (odd == 1) & (j > FIRST) & (j < cuts - 2)
    feeds = (odd == 0) & (j > FIRST) & (j < cuts - 3)
    passes = (j < cuts - 1) & jnp.logical_not(feeds)
    at_once = passes & jnp.logical_not(skips)

    def along_z(step):
        there = lax.rem(z + step + nz, nz)
        return (lax.rem(there, cuts), (there // cuts) * ny + y, q)

    def along_group(step):
        return (j, e, lax.rem(q + step, groups))

    def along_y(step):
        return (j, (e // ny) * ny + lax.rem(y + step, ny), q)

    def local(src, dst, sem):
        return pltpu.make_async_copy(src, dst, sem)

    def remote(src, dst, send, recv, device):
        return pltpu.make_async_remote_copy(src_ref=src, dst_ref=dst, send_sem=send, recv_sem=recv, device_id=device, device_id_type=MESH)

    loads = [local(t_hbm.at[0, k], tb.at[k], load.at[k]) for k in range(count)]
    loads.append(local(s_hbm.at[0], sb, load.at[count]))
    loads.append(local(c_hbm, coup, load.at[count + 1]))
    loads.append(local(strength_hbm, strength, load.at[count + 2]))
    loads.append(local(shift_hbm, shift, load.at[count + 3]))
    for k in (count, *range(1, count), 0, count + 1, count + 2, count + 3):
        loads[k].start()

    barrier = pltpu.get_barrier_semaphore()
    near = [along_z(1), along_z(-1)] + [along_group(r) for r in range(1, groups)] + [along_y(r) for r in range(1, ny)]
    for device in near:
        pl.semaphore_signal(barrier, inc=1, device_id=device, device_id_type=MESH)
    pl.semaphore_wait(barrier, len(near))

    def greet(rnd):
        pl.semaphore_signal(up_sem.at[rnd], inc=1, device_id=along_z(2**rnd), device_id_type=MESH)
        pl.semaphore_signal(dn_sem.at[rnd], inc=1, device_id=along_z(-(2**rnd)), device_id_type=MESH)

    def met(rnd):
        pl.semaphore_wait(up_sem.at[rnd], 1)
        pl.semaphore_wait(dn_sem.at[rnd], 1)

    greet(0)

    loads[count].wait()
    for k in range(count):
        lt[k] = sb[pl.ds(k * orbs, orbs), :].T
    loads[1].wait()
    ah[...], al[...] = halves(tb[1])
    high, low = halves(lt[0])
    lt[1] = lt[1] + (nt(high, ah[...]) + (nt(low, ah[...]) + nt(high, al[...])))
    loads[2].wait()
    bh[...], bl[...] = halves(tb[2])
    high, low = halves(lt[1])
    lt[2] = lt[2] + (nt(high, bh[...]) + (nt(low, bh[...]) + nt(high, bl[...])))

    def piece(p):
        rows = pl.ds(pl.multiple_of(p * width, width), width)
        return rows, remote(gt.at[2, rows], xt.at[rows], xs_sem.at[p], xr_sem.at[p], along_z(1))

    def leap(p):
        rows = pl.ds(pl.multiple_of(p * width, width), width)
        return remote(gt.at[2, rows], xt.at[rows], ls_sem.at[p], xr_sem.at[p], along_z(2))

    def quarter(half, i):
        size = orbs // 4
        return pl.ds(pl.multiple_of((2 * half + i) * size, size), size)

    def share(half):
        rows = [quarter(half, i) for i in range(2)]
        partner = (j, e, q + 1 - 2 * core)
        return [remote(cin.at[rows[i]], cin.at[rows[i]], ps_sem.at[i], pr_sem.at[i], partner) for i in range(2)]

    feed = [remote(p1.at[quarter(core, i)], cin.at[quarter(core, i)], cs_sem.at[i], cr_sem.at[i], along_z(1)) for i in range(2)]
    feed.append(remote(lt.at[2], oin, cs_sem.at[2], cr_sem.at[2], along_z(1)))

    @pl.when(j == 0)
    def _():
        gt[2] = lt[2]

        def send(p, _):
            piece(p)[1].start()
            return 0

        lax.fori_loop(0, PIECES, send, 0)
        gt[0] = lt[0]
        gt[1] = lt[1]

    met(0)
    greet(1)

    loads[0].wait()
    t0h[...], t0l[...] = halves(tb[0].T)
    p1[...] = nt(t0h[...], ah[...]) + (nt(t0l[...], ah[...]) + nt(t0h[...], al[...]))
    p1h[...], p1l[...] = halves(p1[...])
    met(1)
    greet(2)
    p1[...] = nt(p1h[...], bh[...]) + (nt(p1l[...], bh[...]) + nt(p1h[...], bl[...]))
    ch[...], cl[...] = halves(p1[...])
    @pl.when(feeds)
    def _():
        for copy in feed:
            copy.start()

    @pl.when(j >= 4)
    def _():
        met(2)
        greet(3)

    loads[count + 1].wait()

    @pl.when(fed)
    def _():
        given = share(core)
        for i in range(2):
            feed[i].wait_recv()
            given[i].start()
        feed[2].wait_recv()
        high, low = halves(oin[...])
        lt[2] = lt[2] + (nn(high, ch[...]) + (nn(low, ch[...]) + nn(high, cl[...])))
        for copy in share(1 - core):
            copy.wait_recv()
        cih[...], cil[...] = halves(cin[...])
        p1[...] = nn(cih[...], ch[...]) + (nn(cil[...], ch[...]) + nn(cih[...], cl[...]))
        ch[...], cl[...] = halves(p1[...])

    @pl.when(j > 0)
    def _():
        def pass_on(p, _):
            rows, copy = piece(p)
            copy.wait_recv()
            incoming = xt[rows, :]
            rest = incoming - incoming.astype(BF16).astype(F32)
            both = jnp.concatenate([incoming, rest], axis=0).astype(BF16)
            product = nn(both, ch[...]) + nn(both, cl[...])
            gt[2, rows] = lt[2, rows] + (product[:width] + product[width:])

            @pl.when(skips)
            def _():
                leap(p).start()

            @pl.when(at_once)
            def _():
                copy.start()

            return 0

        lax.fori_loop(0, PIECES, pass_on, 0)

        @pl.when(skips)
        def _():
            def late(p, _):
                piece(p)[1].start()
                return 0

            lax.fori_loop(0, PIECES, late, 0)

        @pl.when(fed)
        def _():
            high, low = halves(xt[...])
            xt[...] = oin[...] + (nn(high, cih[...]) + (nn(low, cih[...]) + nn(high, cil[...])))

        high, low = halves(xt[...])
        gt[0] = lt[0] + (nn(high, t0h[...]) + (nn(low, t0h[...]) + nn(high, t0l[...])))
        gt[1] = lt[1] + (nn(high, p1h[...]) + (nn(low, p1h[...]) + nn(high, p1l[...])))

    @pl.when(j < 4)
    def _():
        met(2)
        greet(3)

    part[...] = jnp.zeros_like(part)
    for k in range(count):
        square = gt[k] * gt[k]
        total = jnp.sum(square, axis=0, keepdims=True)
        for i in range(strips):
            part[k * strips + i : k * strips + i + 1, :] = total[:, i * lanes : (i + 1) * lanes]
    sums = [remote(part, ga.at[r - 1], as_sem.at[r - 1], ar_sem.at[r - 1], along_group(r)) for r in range(1, groups)]
    for copy in sums:
        copy.start()
    for k in range(count):
        inner[k] = nn(gt[k].astype(BF16), coup[...])
    loads[count + 2].wait()
    loads[count + 3].wait()

    def weight(target, source):
        total = 0.0
        for m in range(strength.shape[0]):
            total = total + jnp.where(lax.rem(target + shift[m], energies) == source, strength[m], 0.0)
        return total / (cols * groups)

    sources = [(e // ny) * ny + lax.rem(y - r + ny, ny) for r in range(ny)]
    w = [[weight(target, source) for source in sources] for target in (e, lax.rem(e + ny, energies))]

    for copy in sums:
        copy.wait_recv()
    whole = part[...]
    for r in range(1, groups):
        whole = whole + ga[r - 1]
    zs[2] = whole
    dense = [remote(zs.at[2], ys.at[r - 1], ys_sem.at[r - 1], yr_sem.at[r - 1], along_y(r)) for r in range(1, ny)]
    for copy in dense:
        copy.start()
    own = whole * w[0][0]
    other = whole * w[1][0]
    for k in range(count):
        gout[pl.ds(k * orbs, orbs), :] = gt[k].T
    for r in range(1, ny):
        dense[r - 1].wait_recv()
        own = own + ys[r - 1] * w[0][r]
        other = other + ys[r - 1] * w[1][r]
    n = count * strips
    zs[0] = other
    for t, value in enumerate((own, other)):
        eds[t, 0] = value[0:8]
        eds[t, 1] = value[n - 8 : n]
    met(3)
    across = remote(zs.at[0], zr, z_sem.at[0], z_sem.at[1], along_z(cuts))
    across.start()
    down = [remote(eds.at[t, 0], edr.at[t, 1], es_sem.at[t, 0], er_sem.at[t, 1], along_z(t * cuts - 1)) for t in (1, 0)]
    rise = [remote(eds.at[t, 1], edr.at[t, 0], es_sem.at[t, 1], er_sem.at[t, 0], along_z(t * cuts + 1)) for t in (1, 0)]

    @pl.when(j > 0)
    def _():
        for copy in down:
            copy.start()

    @pl.when(j < cuts - 1)
    def _():
        for copy in rise:
            copy.start()

    @pl.when(j == 0)
    def _():
        for t in (0, 1):
            edr[t, 0] = jnp.zeros_like(edr[t, 0])

    @pl.when(j == cuts - 1)
    def _():
        for t in (0, 1):
            edr[t, 1] = jnp.zeros_like(edr[t, 1])

    @pl.when(j > 0)
    def _():
        for copy in rise:
            copy.wait_recv()

    @pl.when(j < cuts - 1)
    def _():
        for copy in down:
            copy.wait_recv()

    across.wait_recv()
    total = own + zr[...]
    left = jnp.concatenate([edr[0, 0, 8 - strips : 8] + edr[1, 0, 8 - strips : 8], total[0 : n - strips]], axis=0)
    right = jnp.concatenate([total[strips:n], edr[0, 1, 0:strips] + edr[1, 1, 0:strips]], axis=0)
    sel[0:n] = total[0:n] + 0.5 * (left + right)

    @pl.when(passes)
    def _():
        def sent(p, _):
            piece(p)[1].wait_send()
            return 0

        lax.fori_loop(0, PIECES, sent, 0)

    @pl.when(skips)
    def _():
        def sent(p, _):
            leap(p).wait_send()
            return 0

        lax.fori_loop(0, PIECES, sent, 0)

    @pl.when(feeds)
    def _():
        for copy in feed:
            copy.wait_send()

    @pl.when(fed)
    def _():
        for copy in share(core):
            copy.wait_send()

    @pl.when(j < cuts - 1)
    def _():
        for copy in rise:
            copy.wait_send()

    @pl.when(j > 0)
    def _():
        for copy in down:
            copy.wait_send()

    for copy in sums + dense + [across]:
        copy.wait_send()


def finish(gin, inner, sel, c_hbm, green, scat, coup, sout, sem):
    count, orbs, lanes = inner.shape[0], inner.shape[2], sel.shape[1]
    strips = orbs // lanes
    stores = [pltpu.make_async_copy(gin, green.at[0], sem.at[count])]
    stores[0].start()
    fetch = pltpu.make_async_copy(c_hbm, coup, sem.at[count + 1])
    fetch.start()
    fetch.wait()
    for k in range(count):
        row = jnp.concatenate([sel[k * strips + i : k * strips + i + 1, :] for i in range(strips)], axis=1)
        rows = pl.ds(k * orbs, orbs)
        sout[rows, :] = nt(coup[...], (inner[k] * row).astype(BF16))
        stores.append(pltpu.make_async_copy(sout.at[rows], scat.at[0, rows], sem.at[k]))
        stores[-1].start()
    for copy in stores:
        copy.wait()


def body(sizes, transfer, source, coupling, strength, mode_shift):
    cuts, energies, groups = sizes
    count, orbs = transfer.shape[1], transfer.shape[2]
    rows, cols = source.shape[1], source.shape[2]
    ny = energies // HALVES
    lanes = 128
    vmem = pltpu.VMEM
    dma = pltpu.SemaphoreType.DMA
    small = 16
    hbm = pl.BlockSpec(memory_space=pltpu.HBM)
    in_vmem = pl.BlockSpec(memory_space=pltpu.VMEM)
    struct = jax.ShapeDtypeStruct
    coupled = [vmem((orbs, orbs), BF16)]
    green, inner, sel = pl.pallas_call(
        functools.partial(kernel, (cuts, energies, groups, count)),
        out_shape=(struct((rows, cols), F32), struct((count, cols, orbs), F32), struct((small, lanes), F32)),
        in_specs=[hbm] * 5,
        out_specs=(in_vmem, in_vmem, in_vmem),
        scratch_shapes=[
            pltpu.SMEM(strength.shape, F32),
            pltpu.SMEM(mode_shift.shape, jnp.int32),
            *coupled,
            vmem((count, orbs, orbs), F32),
            vmem((rows, cols), F32),
            *[vmem((orbs, orbs), BF16) for _ in range(10)],
            vmem((orbs, orbs), F32),
            vmem((orbs, orbs), F32),
            vmem((orbs, orbs), BF16),
            vmem((orbs, orbs), BF16),
            vmem((cols, orbs), F32),
            vmem((count, cols, orbs), F32),
            vmem((cols, orbs), F32),
            vmem((count, cols, orbs), F32),
            vmem((small, lanes), F32),
            vmem((groups - 1, small, lanes), F32),
            vmem((ny - 1, small, lanes), F32),
            vmem((3, small, lanes), F32),
            vmem((small, lanes), F32),
            vmem((2, 2, 8, lanes), F32),
            vmem((2, 2, 8, lanes), F32),
            dma((count + 4,)),
            dma((PIECES,)),
            dma((PIECES,)),
            dma((groups - 1,)),
            dma((groups - 1,)),
            dma((ny - 1,)),
            dma((ny - 1,)),
            dma((2,)),
            dma((2, 2)),
            dma((2, 2)),
            dma((3,)),
            dma((3,)),
            dma((2,)),
            dma((2,)),
            dma((PIECES,)),
            pltpu.SemaphoreType.REGULAR((4,)),
            pltpu.SemaphoreType.REGULAR((4,)),
        ],
        compiler_params=pltpu.CompilerParams(collective_id=0, has_side_effects=True, vmem_limit_bytes=54000000),
        name="propagate",
    )(*[pltpu.with_memory_space_constraint(a, pltpu.HBM) for a in (transfer, source, coupling, strength, mode_shift)])
    out = struct(source.shape, F32)
    return pl.pallas_call(
        finish,
        out_shape=(out, out),
        in_specs=[in_vmem, in_vmem, in_vmem, hbm],
        out_specs=(hbm, hbm),
        scratch_shapes=[*coupled, vmem((rows, cols), F32), dma((count + 2,))],
        compiler_params=pltpu.CompilerParams(vmem_limit_bytes=16 * 2**20),
        name="finish",
    )(green, inner, sel, coupling)


def solution(mesh):
    sizes = tuple(mesh.shape[name] for name in ("cuts", "energy", "group"))
    in_specs = (P("energy", "cuts", None, None), P("energy", "cuts", "group"), P(), P(), P())
    out_specs = (P("energy", "cuts", "group"), P("energy", "cuts", "group"))
    return jax.shard_map(functools.partial(body, sizes), mesh=mesh, in_specs=in_specs, out_specs=out_specs, check_vma=False)
```

```python
import functools

import jax
import jax.numpy as jnp
from jax import lax
from jax.experimental import pallas as pl
from jax.experimental.pallas import tpu as pltpu
from jax.sharding import PartitionSpec as P

MESH = pl.DeviceIdType.MESH
F32, BF16 = jnp.float32, jnp.bfloat16
PIECES = 16
HALVES = 2
FIRST = 7


def halves(value):
    high = value.astype(BF16)
    return high, (value - high.astype(F32)).astype(BF16)


def nn(left, right):
    return jnp.dot(left, right, preferred_element_type=F32)


def nt(left, right):
    return lax.dot_general(left, right, (((1,), (1,)), ((), ())), preferred_element_type=F32)


def kernel(sizes, t_hbm, s_hbm, c_hbm, strength_hbm, shift_hbm, gout, inner, sel, strength, shift, coup, tb, sb, ah, al, bh, bl, t0h, t0l, p1h, p1l, ch, cl,
           p1, cin, cih, cil, oin, lt, xt, gt, part, ga, ys, zs, zr, eds, edr, edf, load, xs_sem, xr_sem, as_sem, ar_sem, ys_sem, yr_sem, zx_sem, zy_sem, es_sem, er_sem, fs_sem, fr_sem,
           cs_sem, cr_sem, ps_sem, pr_sem, ls_sem, up_sem, dn_sem):
    cuts, energies, groups, count = sizes
    ny = energies // HALVES
    nz = HALVES * cuts
    j, e, q = lax.axis_index("cuts"), lax.axis_index("energy"), lax.axis_index("group")
    y = lax.rem(e, ny)
    z = (e // ny) * cuts + j
    orbs, cols = tb.shape[1], xt.shape[0]
    lanes = part.shape[1]
    strips = orbs // lanes
    width = cols // PIECES
    core = lax.rem(q, 2)
    odd = lax.rem(j, 2)
    skips = (odd == 1) & (j >= FIRST) & (j < cuts - 4)
    fed = (odd == 1) & (j > FIRST) & (j < cuts - 2)
    feeds = (odd == 0) & (j > FIRST) & (j < cuts - 3)
    passes = (j < cuts - 1) & jnp.logical_not(feeds)
    at_once = passes & jnp.logical_not(skips)

    def along_z(step, turn=0):
        there = lax.rem(z + step + nz, nz)
        return (lax.rem(there, cuts), (there // cuts) * ny + lax.rem(y + turn, ny), q)

    def along_group(step):
        return (j, e, lax.rem(q + step, groups))

    def along_y(step):
        return (j, (e // ny) * ny + lax.rem(y + step, ny), q)

    def local(src, dst, sem):
        return pltpu.make_async_copy(src, dst, sem)

    def remote(src, dst, send, recv, device):
        return pltpu.make_async_remote_copy(src_ref=src, dst_ref=dst, send_sem=send, recv_sem=recv, device_id=device, device_id_type=MESH)

    loads = [local(t_hbm.at[0, k], tb.at[k], load.at[k]) for k in range(count)]
    loads.append(local(s_hbm.at[0], sb, load.at[count]))
    loads.append(local(c_hbm, coup, load.at[count + 1]))
    loads.append(local(strength_hbm, strength, load.at[count + 2]))
    loads.append(local(shift_hbm, shift, load.at[count + 3]))
    for k in (count, *range(1, count), 0, count + 1, count + 2, count + 3):
        loads[k].start()

    barrier = pltpu.get_barrier_semaphore()
    near = [along_z(1), along_z(-1)] + [along_group(r) for r in range(1, groups)] + [along_y(r) for r in range(1, ny)]
    for device in near:
        pl.semaphore_signal(barrier, inc=1, device_id=device, device_id_type=MESH)
    pl.semaphore_wait(barrier, len(near))

    def greet(rnd):
        reach = 2 ** max(rnd - 1, 0)
        pl.semaphore_signal(up_sem.at[rnd], inc=1, device_id=along_z(reach), device_id_type=MESH)
        pl.semaphore_signal(dn_sem.at[rnd], inc=1, device_id=along_z(-reach), device_id_type=MESH)

    def met(rnd):
        pl.semaphore_wait(up_sem.at[rnd], 1)
        pl.semaphore_wait(dn_sem.at[rnd], 1)

    greet(0)

    loads[count].wait()
    for k in range(count):
        lt[k] = sb[pl.ds(k * orbs, orbs), :].T
    met(0)
    greet(1)
    loads[1].wait()
    ah[...], al[...] = halves(tb[1])
    high, low = halves(lt[0])
    lt[1] = lt[1] + (nt(high, ah[...]) + (nt(low, ah[...]) + nt(high, al[...])))
    loads[2].wait()
    bh[...], bl[...] = halves(tb[2])
    high, low = halves(lt[1])
    lt[2] = lt[2] + (nt(high, bh[...]) + (nt(low, bh[...]) + nt(high, bl[...])))

    def piece(p):
        rows = pl.ds(pl.multiple_of(p * width, width), width)
        return rows, remote(gt.at[2, rows], xt.at[rows], xs_sem.at[p], xr_sem.at[p], along_z(1))

    def leap(p):
        rows = pl.ds(pl.multiple_of(p * width, width), width)
        return remote(gt.at[2, rows], xt.at[rows], ls_sem.at[p], xr_sem.at[p], along_z(2))

    def quarter(half, i):
        size = orbs // 4
        return pl.ds(pl.multiple_of((2 * half + i) * size, size), size)

    def share(half):
        rows = [quarter(half, i) for i in range(2)]
        partner = (j, e, q + 1 - 2 * core)
        return [remote(cin.at[rows[i]], cin.at[rows[i]], ps_sem.at[i], pr_sem.at[i], partner) for i in range(2)]

    feed = [remote(p1.at[quarter(core, i)], cin.at[quarter(core, i)], cs_sem.at[i], cr_sem.at[i], along_z(1)) for i in range(2)]
    feed.append(remote(lt.at[2], oin, cs_sem.at[2], cr_sem.at[2], along_z(1)))

    @pl.when(j == 0)
    def _():
        gt[2] = lt[2]

        def send(p, _):
            piece(p)[1].start()
            return 0

        lax.fori_loop(0, PIECES, send, 0)
        gt[0] = lt[0]
        gt[1] = lt[1]

    met(1)
    greet(2)

    loads[0].wait()
    t0h[...], t0l[...] = halves(tb[0].T)
    p1[...] = nt(t0h[...], ah[...]) + (nt(t0l[...], ah[...]) + nt(t0h[...], al[...]))
    p1h[...], p1l[...] = halves(p1[...])
    met(2)
    greet(3)
    p1[...] = nt(p1h[...], bh[...]) + (nt(p1l[...], bh[...]) + nt(p1h[...], bl[...]))
    ch[...], cl[...] = halves(p1[...])
    @pl.when(feeds)
    def _():
        for copy in feed:
            copy.start()

    @pl.when(j >= 4)
    def _():
        met(3)
        greet(4)

    loads[count + 1].wait()

    @pl.when(fed)
    def _():
        given = share(core)
        for i in range(2):
            feed[i].wait_recv()
            given[i].start()
        feed[2].wait_recv()
        high, low = halves(oin[...])
        lt[2] = lt[2] + (nn(high, ch[...]) + (nn(low, ch[...]) + nn(high, cl[...])))
        for copy in share(1 - core):
            copy.wait_recv()
        cih[...], cil[...] = halves(cin[...])
        p1[...] = nn(cih[...], ch[...]) + (nn(cil[...], ch[...]) + nn(cih[...], cl[...]))
        ch[...], cl[...] = halves(p1[...])

    @pl.when(j > 0)
    def _():
        def pass_on(p, _):
            rows, copy = piece(p)
            copy.wait_recv()
            incoming = xt[rows, :]
            rest = incoming - incoming.astype(BF16).astype(F32)
            both = jnp.concatenate([incoming, rest], axis=0).astype(BF16)
            product = nn(both, ch[...]) + nn(both, cl[...])
            gt[2, rows] = lt[2, rows] + (product[:width] + product[width:])

            @pl.when(skips)
            def _():
                leap(p).start()

            @pl.when(at_once)
            def _():
                copy.start()

            return 0

        lax.fori_loop(0, PIECES, pass_on, 0)

        @pl.when(skips)
        def _():
            def late(p, _):
                piece(p)[1].start()
                return 0

            lax.fori_loop(0, PIECES, late, 0)

        @pl.when(fed)
        def _():
            high, low = halves(xt[...])
            xt[...] = oin[...] + (nn(high, cih[...]) + (nn(low, cih[...]) + nn(high, cil[...])))

        high, low = halves(xt[...])
        gt[0] = lt[0] + (nn(high, t0h[...]) + (nn(low, t0h[...]) + nn(high, t0l[...])))
        gt[1] = lt[1] + (nn(high, p1h[...]) + (nn(low, p1h[...]) + nn(high, p1l[...])))

    @pl.when(j < 4)
    def _():
        met(3)
        greet(4)

    part[...] = jnp.zeros_like(part)
    for k in range(count):
        square = gt[k] * gt[k]
        total = jnp.sum(square, axis=0, keepdims=True)
        for i in range(strips):
            part[k * strips + i : k * strips + i + 1, :] = total[:, i * lanes : (i + 1) * lanes]
    sums = [remote(part, ga.at[r - 1], as_sem.at[r - 1], ar_sem.at[r - 1], along_group(r)) for r in range(1, groups)]
    for copy in sums:
        copy.start()
    for k in range(count):
        inner[k] = nn(gt[k].astype(BF16), coup[...])
    loads[count + 2].wait()
    loads[count + 3].wait()

    def weight(target, source):
        total = 0.0
        for m in range(strength.shape[0]):
            total = total + jnp.where(lax.rem(target + shift[m], energies) == source, strength[m], 0.0)
        return total / (cols * groups)

    below = [lax.rem(y - r + ny, ny) for r in range(ny)]
    w = [[weight(e, half * ny + place) for place in below] for half in (e // ny, 1 - e // ny)]
    for copy in sums:
        copy.wait_recv()
    whole = part[...]
    for r in range(1, groups):
        whole = whole + ga[r - 1]
    n = count * strips
    zs[...] = whole
    eds[1, 0] = whole[0:8]
    eds[1, 1] = whole[n - 8 : n]
    met(4)
    across = [remote(zs, zr.at[r], zx_sem.at[r], zy_sem.at[r], along_z(cuts, r)) for r in range(ny)]
    for copy in across:
        copy.start()
    down = [remote(eds.at[1, 0], edf.at[r, 1], fs_sem.at[r, 0], fr_sem.at[r, 1], along_z(cuts - 1, r)) for r in range(ny)]
    rise = [remote(eds.at[1, 1], edf.at[r, 0], fs_sem.at[r, 1], fr_sem.at[r, 0], along_z(cuts + 1, r)) for r in range(ny)]
    down.append(remote(eds.at[0, 0], edr.at[1], es_sem.at[0], er_sem.at[1], along_z(-1)))
    rise.append(remote(eds.at[0, 1], edr.at[0], es_sem.at[1], er_sem.at[0], along_z(1)))

    @pl.when(j > 0)
    def _():
        for copy in down[:ny]:
            copy.start()

    @pl.when(j < cuts - 1)
    def _():
        for copy in rise[:ny]:
            copy.start()

    dense = [remote(zs, ys.at[r - 1], ys_sem.at[r - 1], yr_sem.at[r - 1], along_y(r)) for r in range(1, ny)]
    for copy in dense:
        copy.start()
    for k in range(count):
        gout[pl.ds(k * orbs, orbs), :] = gt[k].T
    own = whole * w[0][0]
    for r in range(1, ny):
        dense[r - 1].wait_recv()
        own = own + ys[r - 1] * w[0][r]
    eds[0, 0] = own[0:8]
    eds[0, 1] = own[n - 8 : n]

    @pl.when(j > 0)
    def _():
        down[ny].start()

    @pl.when(j < cuts - 1)
    def _():
        rise[ny].start()

    @pl.when(j == 0)
    def _():
        edr[0] = jnp.zeros_like(edr[0])
        for r in range(ny):
            edf[r, 0] = jnp.zeros_like(edf[r, 0])

    @pl.when(j == cuts - 1)
    def _():
        edr[1] = jnp.zeros_like(edr[1])
        for r in range(ny):
            edf[r, 1] = jnp.zeros_like(edf[r, 1])

    @pl.when(j > 0)
    def _():
        for copy in rise:
            copy.wait_recv()

    @pl.when(j < cuts - 1)
    def _():
        for copy in down:
            copy.wait_recv()

    before, after = edr[0], edr[1]
    total = own
    for r in range(ny):
        across[r].wait_recv()
        total = total + zr[r] * w[1][r]
        before = before + edf[r, 0] * w[1][r]
        after = after + edf[r, 1] * w[1][r]
    left = jnp.concatenate([before[8 - strips : 8], total[0 : n - strips]], axis=0)
    right = jnp.concatenate([total[strips:n], after[0:strips]], axis=0)
    sel[0:n] = total[0:n] + 0.5 * (left + right)

    @pl.when(passes)
    def _():
        def sent(p, _):
            piece(p)[1].wait_send()
            return 0

        lax.fori_loop(0, PIECES, sent, 0)

    @pl.when(skips)
    def _():
        def sent(p, _):
            leap(p).wait_send()
            return 0

        lax.fori_loop(0, PIECES, sent, 0)

    @pl.when(feeds)
    def _():
        for copy in feed:
            copy.wait_send()

    @pl.when(fed)
    def _():
        for copy in share(core):
            copy.wait_send()

    @pl.when(j < cuts - 1)
    def _():
        for copy in rise:
            copy.wait_send()

    @pl.when(j > 0)
    def _():
        for copy in down:
            copy.wait_send()

    for copy in sums + dense + across:
        copy.wait_send()


def finish(gin, inner, sel, coup, green, scat, sout, sem):
    count, orbs, lanes = inner.shape[0], inner.shape[2], sel.shape[1]
    strips = orbs // lanes
    stores = [pltpu.make_async_copy(gin, green.at[0], sem.at[count])]
    stores[0].start()
    for k in range(count):
        row = jnp.concatenate([sel[k * strips + i : k * strips + i + 1, :] for i in range(strips)], axis=1)
        rows = pl.ds(k * orbs, orbs)
        sout[rows, :] = nt(coup[...], (inner[k] * row).astype(BF16))
        stores.append(pltpu.make_async_copy(sout.at[rows], scat.at[0, rows], sem.at[k]))
        stores[-1].start()
    for copy in stores:
        copy.wait()


def body(sizes, transfer, source, coupling, strength, mode_shift):
    cuts, energies, groups = sizes
    count, orbs = transfer.shape[1], transfer.shape[2]
    rows, cols = source.shape[1], source.shape[2]
    ny = energies // HALVES
    lanes = 128
    vmem = pltpu.VMEM
    dma = pltpu.SemaphoreType.DMA
    small = 16
    hbm = pl.BlockSpec(memory_space=pltpu.HBM)
    in_vmem = pl.BlockSpec(memory_space=pltpu.VMEM)
    struct = jax.ShapeDtypeStruct
    coupled = [vmem((orbs, orbs), BF16)]
    green, inner, sel = pl.pallas_call(
        functools.partial(kernel, (cuts, energies, groups, count)),
        out_shape=(struct((rows, cols), F32), struct((count, cols, orbs), F32), struct((small, lanes), F32)),
        in_specs=[hbm] * 5,
        out_specs=(in_vmem, in_vmem, in_vmem),
        scratch_shapes=[
            pltpu.SMEM(strength.shape, F32),
            pltpu.SMEM(mode_shift.shape, jnp.int32),
            *coupled,
            vmem((count, orbs, orbs), F32),
            vmem((rows, cols), F32),
            *[vmem((orbs, orbs), BF16) for _ in range(10)],
            vmem((orbs, orbs), F32),
            vmem((orbs, orbs), F32),
            vmem((orbs, orbs), BF16),
            vmem((orbs, orbs), BF16),
            vmem((cols, orbs), F32),
            vmem((count, cols, orbs), F32),
            vmem((cols, orbs), F32),
            vmem((count, cols, orbs), F32),
            vmem((small, lanes), F32),
            vmem((groups - 1, small, lanes), F32),
            vmem((ny - 1, small, lanes), F32),
            vmem((small, lanes), F32),
            vmem((ny, small, lanes), F32),
            vmem((2, 2, 8, lanes), F32),
            vmem((2, 8, lanes), F32),
            vmem((ny, 2, 8, lanes), F32),
            dma((count + 4,)),
            dma((PIECES,)),
            dma((PIECES,)),
            dma((groups - 1,)),
            dma((groups - 1,)),
            dma((ny - 1,)),
            dma((ny - 1,)),
            dma((ny,)),
            dma((ny,)),
            dma((2,)),
            dma((2,)),
            dma((ny, 2)),
            dma((ny, 2)),
            dma((3,)),
            dma((3,)),
            dma((2,)),
            dma((2,)),
            dma((PIECES,)),
            pltpu.SemaphoreType.REGULAR((5,)),
            pltpu.SemaphoreType.REGULAR((5,)),
        ],
        compiler_params=pltpu.CompilerParams(collective_id=0, has_side_effects=True, vmem_limit_bytes=54000000),
        name="propagate",
    )(*[pltpu.with_memory_space_constraint(a, pltpu.HBM) for a in (transfer, source, coupling, strength, mode_shift)])
    out = struct(source.shape, F32)
    return pl.pallas_call(
        finish,
        out_shape=(out, out),
        in_specs=[in_vmem] * 4,
        out_specs=(hbm, hbm),
        scratch_shapes=[vmem((rows, cols), F32), dma((count + 1,))],
        compiler_params=pltpu.CompilerParams(vmem_limit_bytes=16 * 2**20),
        name="finish",
    )(green, inner, sel, coupling)


def solution(mesh):
    sizes = tuple(mesh.shape[name] for name in ("cuts", "energy", "group"))
    in_specs = (P("energy", "cuts", None, None), P("energy", "cuts", "group"), P(), P(), P())
    out_specs = (P("energy", "cuts", "group"), P("energy", "cuts", "group"))
    return jax.shard_map(functools.partial(body, sizes), mesh=mesh, in_specs=in_specs, out_specs=out_specs, check_vma=False)
```

```python
import functools

import jax
import jax.numpy as jnp
from jax import lax
from jax.experimental import pallas as pl
from jax.experimental.pallas import tpu as pltpu
from jax.sharding import PartitionSpec as P

MESH = pl.DeviceIdType.MESH
F32, BF16 = jnp.float32, jnp.bfloat16
PIECES = 16
HALVES = 2
FIRST = 7


def halves(value):
    high = value.astype(BF16)
    return high, (value - high.astype(F32)).astype(BF16)


def nn(left, right):
    return jnp.dot(left, right, preferred_element_type=F32)


def nt(left, right):
    return lax.dot_general(left, right, (((1,), (1,)), ((), ())), preferred_element_type=F32)


def kernel(sizes, t_hbm, s_hbm, c_hbm, strength_hbm, shift_hbm, gout, inner, sel, strength, shift, coup, tb, sb, ah, al, bh, bl, t0h, t0l, p1h, p1l, ch, cl,
           p1, cin, cih, cil, oin, lt, xt, gt, part, ga, ys, zs, zr, eds, edr, load, xs_sem, xr_sem, as_sem, ar_sem, ys_sem, yr_sem, z_sem, es_sem, er_sem,
           cs_sem, cr_sem, ps_sem, pr_sem, ls_sem, up_sem, dn_sem):
    cuts, energies, groups, count = sizes
    ny = energies // HALVES
    nz = HALVES * cuts
    j, e, q = lax.axis_index("cuts"), lax.axis_index("energy"), lax.axis_index("group")
    y = lax.rem(e, ny)
    z = (e // ny) * cuts + j
    orbs, cols = tb.shape[1], xt.shape[0]
    lanes = part.shape[1]
    strips = orbs // lanes
    width = cols // PIECES
    core = lax.rem(q, 2)
    odd = lax.rem(j, 2)
    skips = (odd == 1) & (j >= FIRST) & (j < cuts - 4)
    fed = (odd == 1) & (j > FIRST) & (j < cuts - 2)
    feeds = (odd == 0) & (j > FIRST) & (j < cuts - 3)
    passes = (j < cuts - 1) & jnp.logical_not(feeds)
    at_once = passes & jnp.logical_not(skips)

    def along_z(step):
        there = lax.rem(z + step + nz, nz)
        return (lax.rem(there, cuts), (there // cuts) * ny + y, q)

    def along_group(step):
        return (j, e, lax.rem(q + step, groups))

    def along_y(step):
        return (j, (e // ny) * ny + lax.rem(y + step, ny), q)

    def local(src, dst, sem):
        return pltpu.make_async_copy(src, dst, sem)

    def remote(src, dst, send, recv, device):
        return pltpu.make_async_remote_copy(src_ref=src, dst_ref=dst, send_sem=send, recv_sem=recv, device_id=device, device_id_type=MESH)

    loads = [local(t_hbm.at[0, k], tb.at[k], load.at[k]) for k in range(count)]
    loads.append(local(s_hbm.at[0], sb, load.at[count]))
    loads.append(local(c_hbm, coup, load.at[count + 1]))
    loads.append(local(strength_hbm, strength, load.at[count + 2]))
    loads.append(local(shift_hbm, shift, load.at[count + 3]))
    for k in (count, *range(1, count), 0, count + 1, count + 2, count + 3):
        loads[k].start()

    barrier = pltpu.get_barrier_semaphore()
    near = [along_z(1), along_z(-1)] + [along_group(r) for r in range(1, groups)] + [along_y(r) for r in range(1, ny)]
    for device in near:
        pl.semaphore_signal(barrier, inc=1, device_id=device, device_id_type=MESH)
    pl.semaphore_wait(barrier, len(near))

    def greet(rnd):
        pl.semaphore_signal(up_sem.at[rnd], inc=1, device_id=along_z(2**rnd), device_id_type=MESH)
        pl.semaphore_signal(dn_sem.at[rnd], inc=1, device_id=along_z(-(2**rnd)), device_id_type=MESH)

    def met(rnd):
        pl.semaphore_wait(up_sem.at[rnd], 1)
        pl.semaphore_wait(dn_sem.at[rnd], 1)

    greet(0)

    loads[count].wait()
    for k in range(count):
        lt[k] = sb[pl.ds(k * orbs, orbs), :].T
    loads[1].wait()
    ah[...], al[...] = halves(tb[1])
    high, low = halves(lt[0])
    lt[1] = lt[1] + (nt(high, ah[...]) + (nt(low, ah[...]) + nt(high, al[...])))
    loads[2].wait()
    bh[...], bl[...] = halves(tb[2])
    high, low = halves(lt[1])
    lt[2] = lt[2] + (nt(high, bh[...]) + (nt(low, bh[...]) + nt(high, bl[...])))

    def piece(p):
        rows = pl.ds(pl.multiple_of(p * width, width), width)
        return rows, remote(gt.at[2, rows], xt.at[rows], xs_sem.at[p], xr_sem.at[p], along_z(1))

    def leap(p):
        rows = pl.ds(pl.multiple_of(p * width, width), width)
        return remote(gt.at[2, rows], xt.at[rows], ls_sem.at[p], xr_sem.at[p], along_z(2))

    def quarter(half, i):
        size = orbs // 4
        return pl.ds(pl.multiple_of((2 * half + i) * size, size), size)

    def share(half):
        rows = [quarter(half, i) for i in range(2)]
        partner = (j, e, q + 1 - 2 * core)
        return [remote(cin.at[rows[i]], cin.at[rows[i]], ps_sem.at[i], pr_sem.at[i], partner) for i in range(2)]

    feed = [remote(p1.at[quarter(core, i)], cin.at[quarter(core, i)], cs_sem.at[i], cr_sem.at[i], along_z(1)) for i in range(2)]
    feed.append(remote(lt.at[2], oin, cs_sem.at[2], cr_sem.at[2], along_z(1)))

    @pl.when(j == 0)
    def _():
        gt[2] = lt[2]

        def send(p, _):
            piece(p)[1].start()
            return 0

        lax.fori_loop(0, PIECES, send, 0)
        gt[0] = lt[0]
        gt[1] = lt[1]

    met(0)
    greet(1)

    loads[0].wait()
    t0h[...], t0l[...] = halves(tb[0].T)
    p1[...] = nt(t0h[...], ah[...]) + (nt(t0l[...], ah[...]) + nt(t0h[...], al[...]))
    p1h[...], p1l[...] = halves(p1[...])
    met(1)
    greet(2)
    p1[...] = nt(p1h[...], bh[...]) + (nt(p1l[...], bh[...]) + nt(p1h[...], bl[...]))
    ch[...], cl[...] = halves(p1[...])
    @pl.when(feeds)
    def _():
        for copy in feed:
            copy.start()

    @pl.when(j >= 4)
    def _():
        met(2)
        greet(3)

    loads[count + 1].wait()

    @pl.when(fed)
    def _():
        given = share(core)
        for i in range(2):
            feed[i].wait_recv()
            given[i].start()
        feed[2].wait_recv()
        high, low = halves(oin[...])
        lt[2] = lt[2] + (nn(high, ch[...]) + (nn(low, ch[...]) + nn(high, cl[...])))
        for copy in share(1 - core):
            copy.wait_recv()
        cih[...], cil[...] = halves(cin[...])
        p1[...] = nn(cih[...], ch[...]) + (nn(cil[...], ch[...]) + nn(cih[...], cl[...]))
        ch[...], cl[...] = halves(p1[...])

    @pl.when(j > 0)
    def _():
        def pass_on(p, _):
            rows, copy = piece(p)
            copy.wait_recv()
            incoming = xt[rows, :]
            rest = incoming - incoming.astype(BF16).astype(F32)
            both = jnp.concatenate([incoming, rest], axis=0).astype(BF16)
            product = nn(both, ch[...]) + nn(both, cl[...])
            gt[2, rows] = lt[2, rows] + (product[:width] + product[width:])

            @pl.when(skips)
            def _():
                leap(p).start()

            @pl.when(at_once)
            def _():
                copy.start()

            return 0

        lax.fori_loop(0, PIECES, pass_on, 0)

        @pl.when(skips)
        def _():
            def late(p, _):
                piece(p)[1].start()
                return 0

            lax.fori_loop(0, PIECES, late, 0)

        @pl.when(fed)
        def _():
            high, low = halves(xt[...])
            xt[...] = oin[...] + (nn(high, cih[...]) + (nn(low, cih[...]) + nn(high, cil[...])))

        high, low = halves(xt[...])
        gt[0] = lt[0] + (nn(high, t0h[...]) + (nn(low, t0h[...]) + nn(high, t0l[...])))
        gt[1] = lt[1] + (nn(high, p1h[...]) + (nn(low, p1h[...]) + nn(high, p1l[...])))

    @pl.when(j < 4)
    def _():
        met(2)
        greet(3)

    for k in range(count):
        square = gt[k] * gt[k]
        total = jnp.sum(square, axis=0, keepdims=True)
        for i in range(strips):
            part[k * strips + i : k * strips + i + 1, :] = total[:, i * lanes : (i + 1) * lanes]
    sums = [remote(part, ga.at[r - 1], as_sem.at[r - 1], ar_sem.at[r - 1], along_group(r)) for r in range(1, groups)]
    for copy in sums:
        copy.start()
    for k in range(count):
        inner[k] = nn(gt[k].astype(BF16), coup[...])
    loads[count + 2].wait()
    loads[count + 3].wait()

    def weight(target, source):
        total = 0.0
        for m in range(strength.shape[0]):
            total = total + jnp.where(lax.rem(target + shift[m], energies) == source, strength[m], 0.0)
        return total / (cols * groups)

    sources = [(e // ny) * ny + lax.rem(y - r + ny, ny) for r in range(ny)]
    w = [[weight(target, source) for source in sources] for target in (e, lax.rem(e + ny, energies))]

    for copy in sums:
        copy.wait_recv()
    whole = part[...]
    for r in range(1, groups):
        whole = whole + ga[r - 1]
    zs[2] = whole
    dense = [remote(zs.at[2], ys.at[r - 1], ys_sem.at[r - 1], yr_sem.at[r - 1], along_y(r)) for r in range(1, ny)]
    for copy in dense:
        copy.start()
    own = whole * w[0][0]
    other = whole * w[1][0]
    for k in range(count):
        gout[pl.ds(k * orbs, orbs), :] = gt[k].T
    for r in range(1, ny):
        dense[r - 1].wait_recv()
        own = own + ys[r - 1] * w[0][r]
        other = other + ys[r - 1] * w[1][r]
    n = count * strips
    zs[0] = other
    for t, value in enumerate((own, other)):
        eds[t, 0] = value[0:strips]
        eds[t, 1] = value[n - strips : n]
    met(3)
    across = remote(zs.at[0], zr, z_sem.at[0], z_sem.at[1], along_z(cuts))
    across.start()
    down = [remote(eds.at[t, 0], edr.at[t, 1], es_sem.at[t, 0], er_sem.at[t, 1], along_z(t * cuts - 1)) for t in (1, 0)]
    rise = [remote(eds.at[t, 1], edr.at[t, 0], es_sem.at[t, 1], er_sem.at[t, 0], along_z(t * cuts + 1)) for t in (1, 0)]

    @pl.when(j > 0)
    def _():
        for copy in down:
            copy.start()

    @pl.when(j < cuts - 1)
    def _():
        for copy in rise:
            copy.start()

    @pl.when(j == 0)
    def _():
        for t in (0, 1):
            edr[t, 0] = jnp.zeros_like(edr[t, 0])

    @pl.when(j == cuts - 1)
    def _():
        for t in (0, 1):
            edr[t, 1] = jnp.zeros_like(edr[t, 1])

    @pl.when(j > 0)
    def _():
        for copy in rise:
            copy.wait_recv()

    @pl.when(j < cuts - 1)
    def _():
        for copy in down:
            copy.wait_recv()

    across.wait_recv()
    total = own + zr[...]
    left = jnp.concatenate([edr[0, 0] + edr[1, 0], total[0 : n - strips]], axis=0)
    right = jnp.concatenate([total[strips:n], edr[0, 1] + edr[1, 1]], axis=0)
    sel[0:n] = total[0:n] + 0.5 * (left + right)

    @pl.when(passes)
    def _():
        def sent(p, _):
            piece(p)[1].wait_send()
            return 0

        lax.fori_loop(0, PIECES, sent, 0)

    @pl.when(skips)
    def _():
        def sent(p, _):
            leap(p).wait_send()
            return 0

        lax.fori_loop(0, PIECES, sent, 0)

    @pl.when(feeds)
    def _():
        for copy in feed:
            copy.wait_send()

    @pl.when(fed)
    def _():
        for copy in share(core):
            copy.wait_send()

    @pl.when(j < cuts - 1)
    def _():
        for copy in rise:
            copy.wait_send()

    @pl.when(j > 0)
    def _():
        for copy in down:
            copy.wait_send()

    for copy in sums + dense + [across]:
        copy.wait_send()


def finish(gin, inner, sel, coup, green, scat, sout, sem):
    count, orbs, lanes = inner.shape[0], inner.shape[2], sel.shape[1]
    strips = orbs // lanes
    stores = [pltpu.make_async_copy(gin, green.at[0], sem.at[count])]
    stores[0].start()
    for k in range(count):
        row = jnp.concatenate([sel[k * strips + i : k * strips + i + 1, :] for i in range(strips)], axis=1)
        rows = pl.ds(k * orbs, orbs)
        sout[rows, :] = nt(coup[...], (inner[k] * row).astype(BF16))
        stores.append(pltpu.make_async_copy(sout.at[rows], scat.at[0, rows], sem.at[k]))
        stores[-1].start()
    for copy in stores:
        copy.wait()


def body(sizes, transfer, source, coupling, strength, mode_shift):
    cuts, energies, groups = sizes
    count, orbs = transfer.shape[1], transfer.shape[2]
    rows, cols = source.shape[1], source.shape[2]
    ny = energies // HALVES
    lanes = 128
    vmem = pltpu.VMEM
    dma = pltpu.SemaphoreType.DMA
    small = count * orbs // lanes
    hbm = pl.BlockSpec(memory_space=pltpu.HBM)
    in_vmem = pl.BlockSpec(memory_space=pltpu.VMEM)
    struct = jax.ShapeDtypeStruct
    coupled = [vmem((orbs, orbs), BF16)]
    green, inner, sel = pl.pallas_call(
        functools.partial(kernel, (cuts, energies, groups, count)),
        out_shape=(struct((rows, cols), F32), struct((count, cols, orbs), F32), struct((small, lanes), F32)),
        in_specs=[hbm] * 5,
        out_specs=(in_vmem, in_vmem, in_vmem),
        scratch_shapes=[
            pltpu.SMEM(strength.shape, F32),
            pltpu.SMEM(mode_shift.shape, jnp.int32),
            *coupled,
            vmem((count, orbs, orbs), F32),
            vmem((rows, cols), F32),
            *[vmem((orbs, orbs), BF16) for _ in range(10)],
            vmem((orbs, orbs), F32),
            vmem((orbs, orbs), F32),
            vmem((orbs, orbs), BF16),
            vmem((orbs, orbs), BF16),
            vmem((cols, orbs), F32),
            vmem((count, cols, orbs), F32),
            vmem((cols, orbs), F32),
            vmem((count, cols, orbs), F32),
            vmem((small, lanes), F32),
            vmem((groups - 1, small, lanes), F32),
            vmem((ny - 1, small, lanes), F32),
            vmem((3, small, lanes), F32),
            vmem((small, lanes), F32),
            vmem((2, 2, orbs // lanes, lanes), F32),
            vmem((2, 2, orbs // lanes, lanes), F32),
            dma((count + 4,)),
            dma((PIECES,)),
            dma((PIECES,)),
            dma((groups - 1,)),
            dma((groups - 1,)),
            dma((ny - 1,)),
            dma((ny - 1,)),
            dma((2,)),
            dma((2, 2)),
            dma((2, 2)),
            dma((3,)),
            dma((3,)),
            dma((2,)),
            dma((2,)),
            dma((PIECES,)),
            pltpu.SemaphoreType.REGULAR((4,)),
            pltpu.SemaphoreType.REGULAR((4,)),
        ],
        compiler_params=pltpu.CompilerParams(collective_id=0, has_side_effects=True, vmem_limit_bytes=54000000),
        name="propagate",
    )(*[pltpu.with_memory_space_constraint(a, pltpu.HBM) for a in (transfer, source, coupling, strength, mode_shift)])
    out = struct(source.shape, F32)
    return pl.pallas_call(
        finish,
        out_shape=(out, out),
        in_specs=[in_vmem] * 4,
        out_specs=(hbm, hbm),
        scratch_shapes=[vmem((rows, cols), F32), dma((count + 1,))],
        compiler_params=pltpu.CompilerParams(vmem_limit_bytes=16 * 2**20),
        name="finish",
    )(green, inner, sel, coupling)


def solution(mesh):
    sizes = tuple(mesh.shape[name] for name in ("cuts", "energy", "group"))
    in_specs = (P("energy", "cuts", None, None), P("energy", "cuts", "group"), P(), P(), P())
    out_specs = (P("energy", "cuts", "group"), P("energy", "cuts", "group"))
    return jax.shard_map(functools.partial(body, sizes), mesh=mesh, in_specs=in_specs, out_specs=out_specs, check_vma=False)
```
